32 devices in a mesh: row: 8 (over z, y), col: 4 (over x, core).
Axes of the slice: x: 2, y: 2, z: 4, core: 2. Of those that a mesh axis runs over, the one named last changes fastest.
Arguments:
- matrix: bfloat16 [12, 8, 256, 24, 4, 256], P(None, 'row', None, None, 'col'), as said below
- inv_first: bfloat16 [512, 512], replicated, as said below
- inv_second: bfloat16 [512, 512], replicated, as said below
Outputs:
- panels: bfloat16 [12, 8, 256, 1024], P(None, 'row')
- trailing: bfloat16 [12, 8, 256, 24, 4, 256], P(None, 'row', None, None, 'col')
Inputs may be any that keep to these rules, and one draw needn't show every extreme that they name: `matrix`: symmetric: the entry at (i, j) of M equals the entry at (j, i). `inv_first`: lower triangular: entries above the diagonal are zero, diagonal entries are positive. `inv_second`: lower triangular: entries above the diagonal are zero, diagonal entries are positive.
All inputs are finite; a program needn't handle non-finite values.
Results may differ from the reference program's by a relative error of at most 0.0065.
Values may be sent and summed in bfloat16 or wider, within the bound.
No kernel may reach another device: no remote copies, remote signals or barrier semaphores. Data moves between devices by JAX's collectives and lax.ppermute only.
A program may use at most 256 MiB of HBM per device.

```python
import math
import jax
import jax.numpy as jnp
from jax import lax

ORDER = 24576
NB = 512
TB = 256
N_ROW = 8
N_COL = 4


def lower_factor(source_key):
    key_offdiag, key_diagonal = jax.random.split(source_key)
    spread_scale = 0.1 / math.sqrt(NB)
    positions = jnp.arange(NB)
    strictly_below = positions[:, None] > positions[None, :]
    on_diagonal = positions[:, None] == positions[None, :]
    offdiag = jnp.clip(jax.random.normal(key_offdiag, (NB, NB), jnp.float32), -3.0, 3.0) * spread_scale
    diagonal = jax.random.uniform(key_diagonal, (NB,), jnp.float32, 0.15, 0.25)
    result = jnp.where(strictly_below, offdiag, 0.0) + jnp.where(on_diagonal, diagonal[None, :], 0.0)
    return result.astype(jnp.bfloat16)


def draw_matrix(key, part):
    source_key = jax.random.fold_in(key, 7)
    square = jnp.clip(jax.random.normal(source_key, (ORDER, ORDER), jnp.float32), -4.0, 4.0)
    positions = jnp.arange(ORDER)
    on_diagonal = positions[:, None] == positions[None, :]
    symmetric = (square + square.T) * math.sqrt(0.5) + jnp.where(on_diagonal, 2.0, 0.0)
    return symmetric.reshape(ORDER // (TB * N_ROW), N_ROW, TB, ORDER // (TB * N_COL), N_COL, TB).astype(jnp.bfloat16)


def draw_inv_first(key, part):
    return lower_factor(jax.random.fold_in(key, 11))


def draw_inv_second(key, part):
    return lower_factor(jax.random.fold_in(key, 23))


def setup_inputs(seed: int = 0) -> dict:
    splits = jax.random.split(jax.random.key(seed), 4)
    return {
        "matrix": draw_matrix(jax.random.fold_in(splits[3], 71), 0),
        "inv_first": draw_inv_first(jax.random.fold_in(splits[3], 71), 0),
        "inv_second": draw_inv_second(jax.random.fold_in(splits[3], 71), 0),
    }


def factor_panel(source, inverse, step_index):
    columns = lax.slice_in_dim(source, step_index * NB, (step_index + 1) * NB, axis=1)
    product = jnp.dot(columns, inverse.T, preferred_element_type=jnp.float32)
    positions = jnp.arange(ORDER)
    keep_rows = (positions >= (step_index + 1) * NB)[:, None]
    return jnp.where(keep_rows, product, jnp.zeros_like(product)).astype(jnp.bfloat16)


def apply_update(source, factor):
    blocks = source.reshape(ORDER // NB, NB, ORDER)
    pieces = factor.reshape(ORDER // NB, NB, NB)

    def one_piece(operands):
        row_piece, factor_piece = operands
        product = jnp.dot(factor_piece, factor.T, preferred_element_type=jnp.float32)
        return (row_piece.astype(jnp.float32) - product).astype(jnp.bfloat16)

    return lax.map(one_piece, (blocks, pieces)).reshape(ORDER, ORDER)


def reference(matrix, inv_first, inv_second):
    full_matrix = matrix.reshape(ORDER, ORDER)
    factor_first = factor_panel(full_matrix, inv_first, 0)
    updated_once = apply_update(full_matrix, factor_first)
    factor_second = factor_panel(updated_once, inv_second, 1)
    updated_twice = apply_update(updated_once, factor_second)
    positions = jnp.arange(ORDER)
    inside = positions >= 2 * NB
    tile_index = positions // TB
    keep_mask = inside[:, None] & inside[None, :] & (tile_index[:, None] >= tile_index[None, :])
    trailing = jnp.where(keep_mask, updated_twice, jnp.zeros_like(updated_twice))
    panels = jnp.concatenate([factor_first, factor_second], axis=1)
    panels = panels.reshape(ORDER // (TB * N_ROW), N_ROW, TB, 2 * NB)
    return panels, trailing.reshape(matrix.shape)
```

```python
import jax
import jax.numpy as jnp
from jax import lax
from jax.experimental import pallas as pl
from jax.experimental.pallas import tpu as pltpu
from jax.sharding import PartitionSpec as P

F32 = jnp.float32
BF16 = jnp.bfloat16
LANES = 128
SUB = 8
VMEM_LIMIT = 60 * 1024 * 1024


def from_root(value, axis, source):
    kept = jnp.where(lax.axis_index(axis) == source, value, 0).astype(value.dtype)
    return lax.psum(kept, axis)


def outer_minus(target, left_rows, right_rows):
    product = lax.dot_general(
        left_rows, right_rows, (((1,), (1,)), ((), ())), preferred_element_type=jnp.float32
    )
    return (target.astype(jnp.float32) - product).astype(jnp.bfloat16)


def panel_columns(first_tile, step_index):
    halves = []
    for half_index in range(2):
        halves.append(from_root(first_tile, "col", 2 * step_index + half_index))
    return jnp.concatenate(halves, axis=1)


def column_factor(row_factor, col_id, row_count, col_count):
    owner_count = row_count // col_count
    received = []
    for owner_slot in range(owner_count):
        received.append(from_root(row_factor, "row", owner_slot * col_count + col_id))
    gathered = jnp.stack(received, axis=1)
    return gathered.reshape(-1, gathered.shape[-1])


def local_any(matrix, inv_first, inv_second):
    row_count = lax.axis_size("row")
    col_count = lax.axis_size("col")
    row_id = lax.axis_index("row")
    col_id = lax.axis_index("col")
    tile_rows = matrix.shape[0]
    tile_size = matrix.shape[2]
    tile_cols = matrix.shape[3]
    width = inv_first.shape[0]
    local_rows = tile_rows * tile_size
    local_cols = tile_cols * tile_size
    current = matrix.reshape(local_rows, local_cols)
    row_position = jnp.arange(local_rows, dtype=jnp.int32)
    global_rows = (
        row_position // tile_size * row_count + row_id
    ) * tile_size + row_position % tile_size
    col_position = jnp.arange(local_cols, dtype=jnp.int32)
    global_cols = (
        col_position // tile_size * col_count + col_id
    ) * tile_size + col_position % tile_size

    def factor_rows(first_tile, inverse, step_index):
        columns = panel_columns(first_tile, step_index)
        product = lax.dot_general(
            columns, inverse, (((1,), (1,)), ((), ())), preferred_element_type=jnp.float32
        )
        keep_rows = (global_rows >= (step_index + 1) * width)[:, None]
        return jnp.where(keep_rows, product, jnp.zeros_like(product)).astype(jnp.bfloat16)

    def spread_columns(row_factor):
        shaped = row_factor.reshape(tile_rows, tile_size, width)
        return column_factor(shaped, col_id, row_count, col_count)

    row_first = factor_rows(current[:, :tile_size], inv_first, 0)
    col_first = spread_columns(row_first)
    updated = outer_minus(current, row_first, col_first)
    row_second = factor_rows(updated[:, :tile_size], inv_second, 1)
    col_second = spread_columns(row_second)
    result = outer_minus(updated, row_second, col_second)
    row_tiles = global_rows // tile_size
    col_tiles = global_cols // tile_size
    keep_mask = (
        (global_rows >= 2 * width)[:, None]
        & (global_cols >= 2 * width)[None, :]
        & (row_tiles[:, None] >= col_tiles[None, :])
    )
    trailing = jnp.where(keep_mask, result, jnp.zeros_like(result))
    panels = jnp.concatenate([row_first, row_second], axis=1)
    return (panels.reshape(tile_rows, 1, tile_size, 2 * width), trailing.reshape(matrix.shape))


def dot(left, right):
    return lax.dot_general(left, right, (((1,), (0,)), ((), ())), preferred_element_type=F32)


def link_kernel(ids, mine, other, inv0t, low, lowt):
    slot, plane, core = ids[0] % 4, ids[1] // 2, ids[1] % 2
    tile = mine.shape[1]

    def piece(panel_tile, owner):
        held = slot ^ panel_tile
        return jnp.where(core == owner, mine[held].astype(F32), other[held].astype(F32))

    @pl.when(plane == 0)
    def _():
        rows = [jnp.concatenate([piece(2 + i, j) for j in range(2)], axis=1) for i in range(2)]
        block = jnp.concatenate(rows, axis=0)
        result = dot(block.astype(BF16), inv0t[...])
        low[...] = result.astype(BF16)
        lowt[...] = result.T.astype(BF16)

    @pl.when(plane == 1)
    def _():
        rows = [jnp.concatenate([piece(j, i) for i in range(2)], axis=1) for j in range(2)]
        block = jnp.concatenate(rows, axis=0).T
        result = dot(block.astype(BF16), inv0t[...])
        low[...] = result.astype(BF16)
        lowt[...] = result.T.astype(BF16)


def rows_kernel(ids, q0, q1, q2, q3, inv0t, inv1t, lowt, out, buf):
    tile = q0.shape[1]
    width = 2 * tile
    row_id, col_id = ids[0], ids[1]
    for m, ref in enumerate((q0, q1, q2, q3)):
        buf[:, pl.ds(pl.multiple_of((col_id ^ m) * tile, tile), tile)] = ref[0]
    tile_row = pl.program_id(0) * 8 + row_id
    first = dot(buf[:, :width], inv0t[...])
    first = jnp.where(tile_row >= 2, first, 0.0).astype(BF16)
    rest = (buf[:, width:].astype(F32) - dot(first, lowt[...])).astype(BF16)
    second = dot(rest, inv1t[...])
    second = jnp.where(tile_row >= 4, second, 0.0).astype(BF16)
    out[0, :, :width] = first
    out[0, :, width:] = second


def update_kernel(group, ids, *refs):
    pieces, (inv0, inv1, low, factor, matrix), rest = refs[:8], refs[8:13], refs[13:]
    out, raw, cols, acc = rest[-4:]
    step = pl.program_id(0)
    tile = factor.shape[1]
    width = 2 * tile
    row_id, col_id = ids[0], ids[1]

    @pl.when(step == 0)
    def _():
        for m in range(4):
            base = pl.multiple_of(((row_id % 4) ^ m) * tile, tile)
            for s in range(SUB):
                raw[pl.ds(base, tile), s * tile : (s + 1) * tile] = pieces[2 * m + s % 2][s // 2]
        for s in range(SUB):
            tile_col = (group * SUB + s) * 4 + col_id
            span = slice(s * tile, (s + 1) * tile)
            first = dot(inv0[...], raw[:width, span])
            first = jnp.where(tile_col >= 2, first, 0.0).astype(BF16)
            cols[:width, span] = first
            left = (raw[width:, span].astype(F32) - dot(low[...], first)).astype(BF16)
            second = dot(inv1[...], left)
            cols[width:, span] = jnp.where(tile_col >= 4, second, 0.0).astype(BF16)

    tile_row = step * 8 + row_id
    end = jnp.where(tile_row >= 4, (tile_row - col_id) // 4 + 1 - group * SUB, 0)
    begin = 1 if group == 0 else 0

    @pl.when(end <= begin)
    def _():
        out[...] = jnp.zeros_like(out)

    @pl.when(end > begin)
    def _():
        for s in range(begin, SUB):

            @pl.when(s < end)
            def _():
                product = dot(factor[0], cols[:, s * tile : (s + 1) * tile])
                for part in range(tile // LANES):
                    lanes = slice(part * LANES, (part + 1) * LANES)
                    acc[part, pl.ds(s, tile, stride=SUB), :] = product[:, lanes]

        some = 16
        sub = lax.broadcasted_iota(jnp.int32, (some, SUB, LANES), 1)
        keep = (sub >= begin) & (sub < end)

        def finish(i, carry):
            at = pl.multiple_of(i * some, some)
            span = pl.ds(pl.multiple_of(at * SUB, some * SUB), some * SUB)
            for part in range(tile // LANES):
                lanes = slice(part * LANES, (part + 1) * LANES)
                product = acc[part, span, :].reshape(some, SUB, LANES)
                value = matrix[0, pl.ds(at, some), :, lanes].astype(F32) - product
                out[0, pl.ds(at, some), :, lanes] = jnp.where(keep, value, 0.0).astype(BF16)
            return carry

        lax.fori_loop(0, tile // some, finish, 0)


def params():
    return pltpu.CompilerParams(vmem_limit_bytes=VMEM_LIMIT)


def whole(array):
    rank = array.ndim
    return pl.BlockSpec(array.shape, lambda *_: (0,) * rank)


def local(matrix, inv_first, inv_second):
    row_id = lax.axis_index("row")
    col_id = lax.axis_index("col")
    ids = jnp.stack([row_id, col_id]).astype(jnp.int32)
    tiles, _, tile, tile_cols, _, _ = matrix.shape
    width = inv_first.shape[0]
    groups = tile_cols // SUB
    view = matrix.reshape(tiles, tile, tile_cols, tile)
    upper = row_id >= 4

    def move(value, target):
        pairs = []
        for r in range(8):
            for c in range(4):
                to = target(r, c)
                if to is not None:
                    pairs.append((r * 4 + c, to[0] * 4 + to[1]))
        return lax.ppermute(value, ("row", "col"), pairs)

    strip = view[:, :, 0, :]
    swapped = jnp.swapaxes(strip, 1, 2)
    held = jnp.swapaxes(view[0], 0, 1)

    pieces = []
    for group in range(groups):
        lo = slice(group * SUB, (group + 1) * SUB, 2)
        hi = slice(group * SUB + 1, (group + 1) * SUB, 2)
        even, odd = held[lo], held[hi]
        half = slice(group * SUB // 2, (group + 1) * SUB // 2)
        even_up = move(even, lambda r, c: (r + 4, c) if r < 4 else None)
        odd_up = move(swapped[half], lambda r, c: (4 + c, r - 4) if r >= 4 else None)
        even = jnp.where(upper, even_up, even)
        odd = jnp.where(upper, odd_up, odd)
        across_z = lambda r, c: (r ^ 2, c)
        across_y = lambda r, c: (r ^ 1, c)
        even_z, even_y = move(even, across_z), move(even, across_y)
        odd_z, odd_y = move(odd, across_z), move(odd, across_y)
        even_zy, odd_zy = move(even_z, across_y), move(odd_y, across_z)
        pieces.append((even, odd, even_y, odd_y, even_z, odd_z, even_zy, odd_zy))

    strip_1 = move(strip, lambda r, c: (r, c ^ 1))
    strip_2 = move(strip, lambda r, c: (r, c ^ 2))
    strip_3 = move(strip_2, lambda r, c: (r, c ^ 1))

    inv0t, inv1t = inv_first.T, inv_second.T
    mine = jnp.stack([pieces[0][2 * m][0] for m in range(4)])
    other = move(mine, lambda r, c: (r, c ^ 1))
    smem = pl.BlockSpec(memory_space=pltpu.SMEM)
    square = jax.ShapeDtypeStruct((width, width), BF16)
    low, lowt = pl.pallas_call(
        link_kernel,
        in_specs=[smem, whole(mine), whole(other), whole(inv0t)],
        out_specs=[whole(square), whole(square)],
        out_shape=[square, square],
        grid=(1,),
        compiler_params=params(),
        name="link",
    )(ids, mine, other, inv0t)

    block = pl.BlockSpec((1, tile, tile), lambda t: (t, 0, 0))
    panels = pl.pallas_call(
        rows_kernel,
        grid=(tiles,),
        in_specs=[smem, block, block, block, block, whole(inv0t), whole(inv1t), whole(lowt)],
        out_specs=pl.BlockSpec((1, tile, 2 * width), lambda t: (t, 0, 0)),
        out_shape=jax.ShapeDtypeStruct((tiles, tile, 2 * width), BF16),
        scratch_shapes=[pltpu.VMEM((tile, 2 * width), BF16)],
        compiler_params=params(),
        name="rows",
    )(ids, strip, strip_1, strip_2, strip_3, inv0t, inv1t, lowt)

    result = None
    for group in range(groups):
        operands = [ids, *pieces[group], inv_first, inv_second, low, panels, view]
        specs = [smem, *[whole(p) for p in pieces[group]], whole(inv_first), whole(inv_second), whole(low)]
        specs.append(pl.BlockSpec((1, tile, 2 * width), lambda t: (t, 0, 0)))
        specs.append(pl.BlockSpec((1, tile, SUB, tile), lambda t, g=group: (t, 0, g, 0)))
        aliases = {}
        if result is not None:
            aliases = {len(operands): 0}
            operands.append(result)
            specs.append(pl.BlockSpec(memory_space=pl.ANY))

        def kernel(*refs, g=group):
            update_kernel(g, *refs)

        result = pl.pallas_call(
            kernel,
            grid=(tiles,),
            in_specs=specs,
            out_specs=pl.BlockSpec((1, tile, SUB, tile), lambda t, g=group: (t, 0, g, 0)),
            out_shape=jax.ShapeDtypeStruct(view.shape, BF16),
            scratch_shapes=[
                pltpu.VMEM((2 * width, SUB * tile), BF16),
                pltpu.VMEM((2 * width, SUB * tile), BF16),
                pltpu.VMEM((tile // LANES, tile * SUB, LANES), F32),
            ],
            input_output_aliases=aliases,
            compiler_params=params(),
            name="update_%d" % group,
        )(*operands)

    return panels.reshape(tiles, 1, tile, 2 * width), result.reshape(matrix.shape)


def fits(mesh, matrix, inv_first):
    tiles_match = matrix.shape[3] % SUB == 0 and matrix.shape[3] == 2 * matrix.shape[0]
    panel_match = inv_first.shape[0] == 2 * matrix.shape[2]
    return mesh.shape["row"] == 8 and mesh.shape["col"] == 4 and tiles_match and panel_match


def solution(mesh):
    def body(matrix, inv_first, inv_second):
        plan = local if fits(mesh, matrix, inv_first) else local_any
        return plan(matrix, inv_first, inv_second)

    return jax.shard_map(
        body,
        mesh=mesh,
        in_specs=(P(None, "row", None, None, "col", None), P(), P()),
        out_specs=(P(None, "row", None, None), P(None, "row", None, None, "col", None)),
        check_vma=False,
    )
```

```python
import jax
import jax.numpy as jnp
from jax import lax
from jax.experimental import pallas as pl
from jax.experimental.pallas import tpu as pltpu
from jax.sharding import PartitionSpec as P

F32 = jnp.float32
BF16 = jnp.bfloat16
LANES = 128
SUB = 8
VMEM_LIMIT = 60 * 1024 * 1024


def from_root(value, axis, source):
    kept = jnp.where(lax.axis_index(axis) == source, value, 0).astype(value.dtype)
    return lax.psum(kept, axis)


def outer_minus(target, left_rows, right_rows):
    product = lax.dot_general(
        left_rows, right_rows, (((1,), (1,)), ((), ())), preferred_element_type=jnp.float32
    )
    return (target.astype(jnp.float32) - product).astype(jnp.bfloat16)


def panel_columns(first_tile, step_index):
    halves = []
    for half_index in range(2):
        halves.append(from_root(first_tile, "col", 2 * step_index + half_index))
    return jnp.concatenate(halves, axis=1)


def column_factor(row_factor, col_id, row_count, col_count):
    owner_count = row_count // col_count
    received = []
    for owner_slot in range(owner_count):
        received.append(from_root(row_factor, "row", owner_slot * col_count + col_id))
    gathered = jnp.stack(received, axis=1)
    return gathered.reshape(-1, gathered.shape[-1])


def local_any(matrix, inv_first, inv_second):
    row_count = lax.axis_size("row")
    col_count = lax.axis_size("col")
    row_id = lax.axis_index("row")
    col_id = lax.axis_index("col")
    tile_rows = matrix.shape[0]
    tile_size = matrix.shape[2]
    tile_cols = matrix.shape[3]
    width = inv_first.shape[0]
    local_rows = tile_rows * tile_size
    local_cols = tile_cols * tile_size
    current = matrix.reshape(local_rows, local_cols)
    row_position = jnp.arange(local_rows, dtype=jnp.int32)
    global_rows = (
        row_position // tile_size * row_count + row_id
    ) * tile_size + row_position % tile_size
    col_position = jnp.arange(local_cols, dtype=jnp.int32)
    global_cols = (
        col_position // tile_size * col_count + col_id
    ) * tile_size + col_position % tile_size

    def factor_rows(first_tile, inverse, step_index):
        columns = panel_columns(first_tile, step_index)
        product = lax.dot_general(
            columns, inverse, (((1,), (1,)), ((), ())), preferred_element_type=jnp.float32
        )
        keep_rows = (global_rows >= (step_index + 1) * width)[:, None]
        return jnp.where(keep_rows, product, jnp.zeros_like(product)).astype(jnp.bfloat16)

    def spread_columns(row_factor):
        shaped = row_factor.reshape(tile_rows, tile_size, width)
        return column_factor(shaped, col_id, row_count, col_count)

    row_first = factor_rows(current[:, :tile_size], inv_first, 0)
    col_first = spread_columns(row_first)
    updated = outer_minus(current, row_first, col_first)
    row_second = factor_rows(updated[:, :tile_size], inv_second, 1)
    col_second = spread_columns(row_second)
    result = outer_minus(updated, row_second, col_second)
    row_tiles = global_rows // tile_size
    col_tiles = global_cols // tile_size
    keep_mask = (
        (global_rows >= 2 * width)[:, None]
        & (global_cols >= 2 * width)[None, :]
        & (row_tiles[:, None] >= col_tiles[None, :])
    )
    trailing = jnp.where(keep_mask, result, jnp.zeros_like(result))
    panels = jnp.concatenate([row_first, row_second], axis=1)
    return (panels.reshape(tile_rows, 1, tile_size, 2 * width), trailing.reshape(matrix.shape))


def dot(left, right):
    return lax.dot_general(left, right, (((1,), (0,)), ((), ())), preferred_element_type=F32)


def link_kernel(ids, mine, other, inv0t, low, lowt):
    slot, plane, core = ids[0] % 4, ids[1] // 2, ids[1] % 2
    tile = mine.shape[1]

    def piece(panel_tile, owner):
        held = slot ^ panel_tile
        return jnp.where(core == owner, mine[held].astype(F32), other[held].astype(F32))

    @pl.when(plane == 0)
    def _():
        rows = [jnp.concatenate([piece(2 + i, j) for j in range(2)], axis=1) for i in range(2)]
        block = jnp.concatenate(rows, axis=0)
        result = dot(block.astype(BF16), inv0t[...])
        low[...] = result.astype(BF16)
        lowt[...] = result.T.astype(BF16)

    @pl.when(plane == 1)
    def _():
        rows = [jnp.concatenate([piece(j, i) for i in range(2)], axis=1) for j in range(2)]
        block = jnp.concatenate(rows, axis=0).T
        result = dot(block.astype(BF16), inv0t[...])
        low[...] = result.astype(BF16)
        lowt[...] = result.T.astype(BF16)


def rows_kernel(ids, strips, inv0t, inv1t, lowt, out, buf):
    _, count, tile, _ = strips.shape
    width = 2 * tile
    row_id = ids[0]
    for k in range(4):
        for i in range(count):
            buf[i * tile : (i + 1) * tile, k * tile : (k + 1) * tile] = strips[k, i]
    local = lax.broadcasted_iota(jnp.int32, (count * tile, 1), 0) // tile
    tile_row = (pl.program_id(0) * count + local) * 8 + row_id
    first = dot(buf[:, :width], inv0t[...])
    first = jnp.where(tile_row >= 2, first, 0.0).astype(BF16)
    rest = (buf[:, width:].astype(F32) - dot(first, lowt[...])).astype(BF16)
    second = dot(rest, inv1t[...])
    second = jnp.where(tile_row >= 4, second, 0.0).astype(BF16)
    for i in range(count):
        out[i, :, :width] = first[i * tile : (i + 1) * tile]
        out[i, :, width:] = second[i * tile : (i + 1) * tile]


def cols_kernel(start, stride, ids, p0, p1, p2, p3, inv0, inv1, low, out, raw):
    count, tile, _ = p0.shape
    width = 2 * tile
    row_id, col_id = ids[0], ids[1]
    for m, ref in enumerate((p0, p1, p2, p3)):
        base = pl.multiple_of(((row_id % 4) ^ m) * tile, tile)
        for i in range(count):
            raw[pl.ds(base, tile), i * tile : (i + 1) * tile] = ref[i]
    local = lax.broadcasted_iota(jnp.int32, (1, count * tile), 1) // tile
    tile_col = (start + (pl.program_id(0) * count + local) * stride) * 4 + col_id
    first = dot(inv0[...], raw[:width])
    first = jnp.where(tile_col >= 2, first, 0.0).astype(BF16)
    rest = (raw[width:].astype(F32) - dot(low[...], first)).astype(BF16)
    second = dot(inv1[...], rest)
    second = jnp.where(tile_col >= 4, second, 0.0).astype(BF16)
    for i in range(count):
        out[i, :width] = first[:, i * tile : (i + 1) * tile]
        out[i, width:] = second[:, i * tile : (i + 1) * tile]


def zeros_kernel(_, out):
    out[...] = jnp.zeros_like(out)


def update_kernel(group, start, ids, even, odd, factor, matrix, _, out, acc):
    tile = factor.shape[1]
    row_id, col_id = ids[0], ids[1]
    tile_row = (start + pl.program_id(0)) * 8 + row_id
    end = jnp.where(tile_row >= 4, (tile_row - col_id) // 4 + 1 - group * SUB, 0)
    begin = 1 if group == 0 else 0
    held = [(odd if s % 2 else even, s // 2) for s in range(SUB)]

    @pl.when(end <= begin)
    def _():
        out[...] = jnp.zeros_like(out)

    @pl.when(end > begin)
    def _():
        def fill(chosen):
            for s in chosen:
                ref, at = held[s]
                product = dot(factor[0], ref[at])
                for part in range(tile // LANES):
                    lanes = slice(part * LANES, (part + 1) * LANES)
                    acc[part, pl.ds(s, tile, stride=SUB), :] = product[:, lanes]

        @pl.when(end >= SUB)
        def _():
            fill(range(begin, SUB))

        for pair in range(0, len(held), 2):

            @pl.when((end < SUB) & (pair < end))
            def _(pair=pair):
                fill(range(max(pair, begin), pair + 2))

        some = 32
        sub = lax.broadcasted_iota(jnp.int32, (some, SUB, LANES), 1)
        keep = (sub >= begin) & (sub < end)

        def finish(i, carry):
            at = pl.multiple_of(i * some, some)
            span = pl.ds(pl.multiple_of(at * SUB, some * SUB), some * SUB)
            for part in range(tile // LANES):
                lanes = slice(part * LANES, (part + 1) * LANES)
                product = acc[part, span, :].reshape(some, SUB, LANES)
                value = matrix[0, pl.ds(at, some), :, lanes].astype(F32) - product
                out[0, pl.ds(at, some), :, lanes] = jnp.where(keep, value, 0.0).astype(BF16)
            return carry

        lax.fori_loop(0, tile // some, finish, 0)


def params():
    return pltpu.CompilerParams(vmem_limit_bytes=VMEM_LIMIT)


def whole(array):
    rank = array.ndim
    return pl.BlockSpec(array.shape, lambda *_: (0,) * rank)


def local(matrix, inv_first, inv_second):
    row_id = lax.axis_index("row")
    col_id = lax.axis_index("col")
    ids = jnp.stack([row_id, col_id]).astype(jnp.int32)
    tiles, _, tile, tile_cols, _, _ = matrix.shape
    width = inv_first.shape[0]
    groups = tile_cols // SUB
    ratio = tiles // groups
    view = matrix.reshape(tiles, tile, tile_cols, tile)
    upper = row_id >= 4
    smem = pl.BlockSpec(memory_space=pltpu.SMEM)
    inv0t, inv1t = inv_first.T, inv_second.T

    def together(*values):
        return lax.optimization_barrier(values)

    def move(value, target):
        pairs = []
        for r in range(8):
            for c in range(4):
                to = target(r, c)
                if to is not None:
                    pairs.append((r * 4 + c, to[0] * 4 + to[1]))
        return lax.ppermute(value, ("row", "col"), pairs)

    def across_z(value):
        return move(value, lambda r, c: (r ^ 2, c))

    def across_y(value):
        return move(value, lambda r, c: (r ^ 1, c))

    def across_core(value):
        return move(value, lambda r, c: (r, c ^ 1))

    def lift(value):
        return move(value, lambda r, c: (r + 4, c) if r < 4 else None)

    def factor_link(mine, other):
        square = jax.ShapeDtypeStruct((width, width), BF16)
        return pl.pallas_call(
            link_kernel,
            in_specs=[smem, whole(mine), whole(other), whole(inv0t)],
            out_specs=[whole(square), whole(square)],
            out_shape=[square, square],
            grid=(1,),
            compiler_params=params(),
            name="link",
        )(ids, mine, other, inv0t)

    def factor_rows(strips, lowt):
        count = 2
        block = pl.BlockSpec((4, count, tile, tile), lambda t: (0, t, 0, 0))
        return pl.pallas_call(
            rows_kernel,
            grid=(tiles // count,),
            in_specs=[smem, block, whole(inv0t), whole(inv1t), whole(lowt)],
            out_specs=pl.BlockSpec((count, tile, 2 * width), lambda t: (t, 0, 0)),
            out_shape=jax.ShapeDtypeStruct((tiles, tile, 2 * width), BF16),
            scratch_shapes=[pltpu.VMEM((count * tile, 2 * width), BF16)],
            compiler_params=params(),
            cost_estimate=cost(tiles * 6 * tile * width * width, 24 * tiles * tile * tile),
            name="rows",
        )(ids, strips, inv0t, inv1t, lowt)

    def factor_cols(start, pieces, low):
        total = pieces[0].shape[0]
        count = 2
        block = pl.BlockSpec((count, tile, tile), lambda s: (s, 0, 0))

        def kernel(*refs):
            cols_kernel(start, 2, *refs)

        return pl.pallas_call(
            kernel,
            grid=(total // count,),
            in_specs=[smem, *[block] * 4, whole(inv_first), whole(inv_second), whole(low)],
            out_specs=pl.BlockSpec((count, 2 * width, tile), lambda s: (s, 0, 0)),
            out_shape=jax.ShapeDtypeStruct((total, 2 * width, tile), BF16),
            scratch_shapes=[pltpu.VMEM((2 * width, count * tile), BF16)],
            compiler_params=params(),
            cost_estimate=cost(total * 6 * tile * width * width, 24 * total * tile * tile),
            name="cols_%d" % start,
        )(ids, *pieces, inv_first, inv_second, low)

    def cost(flops, size):
        return pl.CostEstimate(flops=flops, bytes_accessed=size, transcendentals=0)

    def clear(gate):
        def place(i):
            group, first = 1, 0
            for g in range(1, groups):
                begin = ratio * g * (g - 1) // 2
                group = jnp.where(i >= begin, g, group)
                first = jnp.where(i >= begin, begin, first)
            return (i - first, 0, group, 0)

        return pl.pallas_call(
            zeros_kernel,
            grid=(ratio * groups * (groups - 1) // 2,),
            in_specs=[smem],
            out_specs=pl.BlockSpec((1, tile, SUB, tile), place),
            out_shape=jax.ShapeDtypeStruct(view.shape, BF16),
            compiler_params=params(),
            cost_estimate=cost(0, tiles * tile * SUB * tile * 2),
            name="clear",
        )(together(ids, gate)[0])

    def update(result, group, start, stop, cols, panels):
        grid_block = pl.BlockSpec((1, tile, SUB, tile), lambda t: (t + start, 0, group, 0))

        def kernel(*refs):
            update_kernel(group, start, *refs)

        return pl.pallas_call(
            kernel,
            grid=(stop - start,),
            in_specs=[
                smem,
                *[whole(part) for part in cols],
                pl.BlockSpec((1, tile, 2 * width), lambda t: (t + start, 0, 0)),
                grid_block,
                pl.BlockSpec(memory_space=pl.ANY),
            ],
            out_specs=grid_block,
            out_shape=jax.ShapeDtypeStruct(view.shape, BF16),
            scratch_shapes=[pltpu.VMEM((tile // LANES, tile * SUB, LANES), F32)],
            input_output_aliases={len(cols) + 3: 0},
            compiler_params=params(),
            cost_estimate=cost(
                (stop - start) * 2 * tile * tile * 2 * width * SUB,
                (stop - start) * 6 * tile * tile * SUB,
            ),
            name="update_%d_%d" % (group, start),
        )(ids, *cols, panels, view, result)

    def cross(value):
        return move(value, lambda r, c: (4 + c, r - 4) if r >= 4 else None)

    count = 2 * groups
    half = SUB // 2
    held = jnp.swapaxes(view[0], 0, 1)
    own = [held[i // 2 * SUB + i % 2 : (i // 2 + 1) * SUB : 2] for i in range(count)]
    up, base, ez, ey, ed, cols = ([None] * count for _ in range(6))

    def begin(i, token):
        got, token = together(up[i], token)
        base[i] = jnp.where(upper, got, own[i])
        ez[i], ey[i] = across_z(base[i]), across_y(base[i])
        return token

    def raise_after(i, gate):
        source, gate = together(own[i], gate)
        up[i] = lift(source)
        return gate

    def cross_after(i, gate):
        source, gate = together(swapped[i // 2 * half : (i // 2 + 1) * half], gate)
        up[i] = cross(source)
        return gate

    def forward(i, token):
        ez[i], token = together(ez[i], token)
        ed[i] = across_y(ez[i])
        return token

    def make_cols(i, gate):
        parts = together(base[i], ey[i], ez[i], ed[i], gate)
        cols[i] = factor_cols(i // 2 * SUB + i % 2, parts[:4], low)

    up[0] = lift(own[0])
    source, own[0] = together(view, own[0])
    strip = source[:, :, 0, :]
    swapped = jnp.swapaxes(strip, 1, 2)
    strips = lax.all_gather(strip, "col")
    up[1] = cross(swapped[:half])
    up[0] = raise_after(2, up[0])
    begin(0, ids)
    up[1] = cross_after(3, up[1])
    result = clear(base[0])
    ey[0] = forward(0, ey[0])
    up[2] = raise_after(4, up[2])
    begin(1, base[0])
    up[3] = cross_after(5, up[3])
    mine = jnp.stack([p[0] for p in (base[0], ey[0], ez[0], ed[0])])
    other = across_core(mine)
    base[1] = begin(2, base[1])
    base[2] = forward(1, base[2])
    low, lowt = factor_link(mine, other)
    low = begin(3, low)
    make_cols(0, base[3])
    cols[0] = forward(2, cols[0])
    make_cols(1, ez[2])
    cols[1] = begin(4, cols[1])
    lowt, base[4] = together(lowt, base[4])
    panels = factor_rows(strips, lowt)
    panels = forward(3, panels)
    result, ez[3] = together(result, ez[3])
    middle = tiles // 2
    result = update(result, 0, 0, middle, cols[0:2], panels)
    result = begin(5, result)
    base[5] = forward(4, base[5])
    make_cols(2, base[5])
    result, cols[2] = together(result, cols[2])
    result = update(result, 0, middle, tiles, cols[0:2], panels)
    ey[5], result = together(ey[5], result)
    ed[5] = across_z(ey[5])
    make_cols(3, ey[5])
    result, cols[3] = together(result, cols[3])
    result = update(result, 1, ratio, tiles, cols[2:4], panels)
    ed[4], result = together(ed[4], result)
    make_cols(4, base[5])
    ed[5], cols[4] = together(ed[5], cols[4])
    make_cols(5, base[5])
    result = update(result, 2, 2 * ratio, tiles, cols[4:6], panels)
    return panels.reshape(tiles, 1, tile, 2 * width), result.reshape(matrix.shape)


def fits(mesh, matrix, inv_first):
    tiles_match = matrix.shape[3] == 3 * SUB and matrix.shape[0] == 12
    panel_match = inv_first.shape[0] == 2 * matrix.shape[2]
    return mesh.shape["row"] == 8 and mesh.shape["col"] == 4 and tiles_match and panel_match


def solution(mesh):
    def body(matrix, inv_first, inv_second):
        plan = local if fits(mesh, matrix, inv_first) else local_any
        return plan(matrix, inv_first, inv_second)

    return jax.shard_map(
        body,
        mesh=mesh,
        in_specs=(P(None, "row", None, None, "col", None), P(), P()),
        out_specs=(P(None, "row", None, None), P(None, "row", None, None, "col", None)),
        check_vma=False,
    )
```

```python
import jax
import jax.numpy as jnp
from jax import lax
from jax.experimental import pallas as pl
from jax.experimental.pallas import tpu as pltpu
from jax.sharding import PartitionSpec as P

F32 = jnp.float32
BF16 = jnp.bfloat16
LANES = 128
SUB = 8
VMEM_LIMIT = 60 * 1024 * 1024


def from_root(value, axis, source):
    kept = jnp.where(lax.axis_index(axis) == source, value, 0).astype(value.dtype)
    return lax.psum(kept, axis)


def outer_minus(target, left_rows, right_rows):
    product = lax.dot_general(
        left_rows, right_rows, (((1,), (1,)), ((), ())), preferred_element_type=jnp.float32
    )
    return (target.astype(jnp.float32) - product).astype(jnp.bfloat16)


def panel_columns(first_tile, step_index):
    halves = []
    for half_index in range(2):
        halves.append(from_root(first_tile, "col", 2 * step_index + half_index))
    return jnp.concatenate(halves, axis=1)


def column_factor(row_factor, col_id, row_count, col_count):
    owner_count = row_count // col_count
    received = []
    for owner_slot in range(owner_count):
        received.append(from_root(row_factor, "row", owner_slot * col_count + col_id))
    gathered = jnp.stack(received, axis=1)
    return gathered.reshape(-1, gathered.shape[-1])


def local_any(matrix, inv_first, inv_second):
    row_count = lax.axis_size("row")
    col_count = lax.axis_size("col")
    row_id = lax.axis_index("row")
    col_id = lax.axis_index("col")
    tile_rows = matrix.shape[0]
    tile_size = matrix.shape[2]
    tile_cols = matrix.shape[3]
    width = inv_first.shape[0]
    local_rows = tile_rows * tile_size
    local_cols = tile_cols * tile_size
    current = matrix.reshape(local_rows, local_cols)
    row_position = jnp.arange(local_rows, dtype=jnp.int32)
    global_rows = (
        row_position // tile_size * row_count + row_id
    ) * tile_size + row_position % tile_size
    col_position = jnp.arange(local_cols, dtype=jnp.int32)
    global_cols = (
        col_position // tile_size * col_count + col_id
    ) * tile_size + col_position % tile_size

    def factor_rows(first_tile, inverse, step_index):
        columns = panel_columns(first_tile, step_index)
        product = lax.dot_general(
            columns, inverse, (((1,), (1,)), ((), ())), preferred_element_type=jnp.float32
        )
        keep_rows = (global_rows >= (step_index + 1) * width)[:, None]
        return jnp.where(keep_rows, product, jnp.zeros_like(product)).astype(jnp.bfloat16)

    def spread_columns(row_factor):
        shaped = row_factor.reshape(tile_rows, tile_size, width)
        return column_factor(shaped, col_id, row_count, col_count)

    row_first = factor_rows(current[:, :tile_size], inv_first, 0)
    col_first = spread_columns(row_first)
    updated = outer_minus(current, row_first, col_first)
    row_second = factor_rows(updated[:, :tile_size], inv_second, 1)
    col_second = spread_columns(row_second)
    result = outer_minus(updated, row_second, col_second)
    row_tiles = global_rows // tile_size
    col_tiles = global_cols // tile_size
    keep_mask = (
        (global_rows >= 2 * width)[:, None]
        & (global_cols >= 2 * width)[None, :]
        & (row_tiles[:, None] >= col_tiles[None, :])
    )
    trailing = jnp.where(keep_mask, result, jnp.zeros_like(result))
    panels = jnp.concatenate([row_first, row_second], axis=1)
    return (panels.reshape(tile_rows, 1, tile_size, 2 * width), trailing.reshape(matrix.shape))


def dot(left, right):
    return lax.dot_general(left, right, (((1,), (0,)), ((), ())), preferred_element_type=F32)


def link_kernel(ids, mine, other, inv0t, low, lowt):
    slot, plane, core = ids[0] % 4, ids[1] // 2, ids[1] % 2
    tile = mine.shape[1]

    def piece(panel_tile, owner):
        held = slot ^ panel_tile
        return jnp.where(core == owner, mine[held].astype(F32), other[held].astype(F32))

    @pl.when(plane == 0)
    def _():
        rows = [jnp.concatenate([piece(2 + i, j) for j in range(2)], axis=1) for i in range(2)]
        block = jnp.concatenate(rows, axis=0)
        result = dot(block.astype(BF16), inv0t[...])
        low[...] = result.astype(BF16)
        lowt[...] = result.T.astype(BF16)

    @pl.when(plane == 1)
    def _():
        rows = [jnp.concatenate([piece(j, i) for i in range(2)], axis=1) for j in range(2)]
        block = jnp.concatenate(rows, axis=0).T
        result = dot(block.astype(BF16), inv0t[...])
        low[...] = result.astype(BF16)
        lowt[...] = result.T.astype(BF16)


def rows_kernel(ids, q0, q1, q2, q3, inv0t, inv1t, lowt, out, buf):
    count, tile, _ = q0.shape
    width = 2 * tile
    row_id, col_id = ids[0], ids[1]
    for m, ref in enumerate((q0, q1, q2, q3)):
        base = pl.multiple_of((col_id ^ m) * tile, tile)
        for i in range(count):
            buf[i * tile : (i + 1) * tile, pl.ds(base, tile)] = ref[i]
    local = lax.broadcasted_iota(jnp.int32, (count * tile, 1), 0) // tile
    tile_row = (pl.program_id(0) * count + local) * 8 + row_id
    first = dot(buf[:, :width], inv0t[...])
    first = jnp.where(tile_row >= 2, first, 0.0).astype(BF16)
    rest = (buf[:, width:].astype(F32) - dot(first, lowt[...])).astype(BF16)
    second = dot(rest, inv1t[...])
    second = jnp.where(tile_row >= 4, second, 0.0).astype(BF16)
    for i in range(count):
        out[i, :, :width] = first[i * tile : (i + 1) * tile]
        out[i, :, width:] = second[i * tile : (i + 1) * tile]


def cols_kernel(start, ids, *refs):
    pieces, (inv0, inv1, low, out, raw) = refs[:8], refs[8:]
    tile = pieces[0].shape[1]
    width = 2 * tile
    row_id, col_id = ids[0], ids[1]
    for m in range(4):
        base = pl.multiple_of(((row_id % 4) ^ m) * tile, tile)
        for i in range(2):
            raw[pl.ds(base, tile), i * tile : (i + 1) * tile] = pieces[2 * m + i][0]
    local = lax.broadcasted_iota(jnp.int32, (1, 2 * tile), 1) // tile
    tile_col = (start + pl.program_id(0) * 2 + local) * 4 + col_id
    first = dot(inv0[...], raw[:width])
    first = jnp.where(tile_col >= 2, first, 0.0).astype(BF16)
    rest = (raw[width:].astype(F32) - dot(low[...], first)).astype(BF16)
    second = dot(inv1[...], rest)
    second = jnp.where(tile_col >= 4, second, 0.0).astype(BF16)
    for i in range(2):
        out[i, :width] = first[:, i * tile : (i + 1) * tile]
        out[i, width:] = second[:, i * tile : (i + 1) * tile]


def zeros_kernel(_, out):
    out[...] = jnp.zeros_like(out)


def update_kernel(group, start, ids, cols, factor, matrix, _, out, acc):
    tile = factor.shape[1]
    row_id, col_id = ids[0], ids[1]
    tile_row = (start + pl.program_id(0)) * 8 + row_id
    end = jnp.where(tile_row >= 4, (tile_row - col_id) // 4 + 1 - group * SUB, 0)
    begin = 1 if group == 0 else 0

    @pl.when(end <= begin)
    def _():
        out[...] = jnp.zeros_like(out)

    @pl.when(end > begin)
    def _():
        def fill(chosen):
            for s in chosen:
                product = dot(factor[0], cols[s])
                for part in range(tile // LANES):
                    lanes = slice(part * LANES, (part + 1) * LANES)
                    acc[part, pl.ds(s, tile, stride=SUB), :] = product[:, lanes]

        @pl.when(end >= SUB)
        def _():
            fill(range(begin, SUB))

        for pair in range(0, SUB, 2):

            @pl.when((end < SUB) & (pair < end))
            def _(pair=pair):
                fill(range(max(pair, begin), pair + 2))

        some = 32
        sub = lax.broadcasted_iota(jnp.int32, (some, SUB, LANES), 1)
        keep = (sub >= begin) & (sub < end)

        def finish(i, carry):
            at = pl.multiple_of(i * some, some)
            span = pl.ds(pl.multiple_of(at * SUB, some * SUB), some * SUB)
            for part in range(tile // LANES):
                lanes = slice(part * LANES, (part + 1) * LANES)
                product = acc[part, span, :].reshape(some, SUB, LANES)
                value = matrix[0, pl.ds(at, some), :, lanes].astype(F32) - product
                out[0, pl.ds(at, some), :, lanes] = jnp.where(keep, value, 0.0).astype(BF16)
            return carry

        lax.fori_loop(0, tile // some, finish, 0)


def params():
    return pltpu.CompilerParams(vmem_limit_bytes=VMEM_LIMIT)


def whole(array):
    rank = array.ndim
    return pl.BlockSpec(array.shape, lambda *_: (0,) * rank)


def local(matrix, inv_first, inv_second):
    row_id = lax.axis_index("row")
    col_id = lax.axis_index("col")
    ids = jnp.stack([row_id, col_id]).astype(jnp.int32)
    tiles, _, tile, tile_cols, _, _ = matrix.shape
    width = inv_first.shape[0]
    groups = tile_cols // SUB
    ratio = tiles // groups
    view = matrix.reshape(tiles, tile, tile_cols, tile)
    upper = row_id >= 4
    smem = pl.BlockSpec(memory_space=pltpu.SMEM)
    inv0t, inv1t = inv_first.T, inv_second.T

    def together(*values):
        return lax.optimization_barrier(values)

    def move(value, target):
        pairs = []
        for r in range(8):
            for c in range(4):
                to = target(r, c)
                if to is not None:
                    pairs.append((r * 4 + c, to[0] * 4 + to[1]))
        return lax.ppermute(value, ("row", "col"), pairs)

    def across_z(value):
        return move(value, lambda r, c: (r ^ 2, c))

    def across_y(value):
        return move(value, lambda r, c: (r ^ 1, c))

    def across_core(value):
        return move(value, lambda r, c: (r, c ^ 1))

    def across_x(value):
        return move(value, lambda r, c: (r, c ^ 2))

    def lift(value):
        return move(value, lambda r, c: (r + 4, c) if r < 4 else None)

    def factor_link(mine, other):
        square = jax.ShapeDtypeStruct((width, width), BF16)
        return pl.pallas_call(
            link_kernel,
            in_specs=[smem, whole(mine), whole(other), whole(inv0t)],
            out_specs=[whole(square), whole(square)],
            out_shape=[square, square],
            grid=(1,),
            compiler_params=params(),
            name="link",
        )(ids, mine, other, inv0t)

    def factor_rows(strips, lowt):
        count = 2
        block = pl.BlockSpec((count, tile, tile), lambda t: (t, 0, 0))
        return pl.pallas_call(
            rows_kernel,
            grid=(tiles // count,),
            in_specs=[smem, *[block] * 4, whole(inv0t), whole(inv1t), whole(lowt)],
            out_specs=pl.BlockSpec((count, tile, 2 * width), lambda t: (t, 0, 0)),
            out_shape=jax.ShapeDtypeStruct((tiles, tile, 2 * width), BF16),
            scratch_shapes=[pltpu.VMEM((count * tile, 2 * width), BF16)],
            compiler_params=params(),
            cost_estimate=cost(tiles * 6 * tile * width * width, 24 * tiles * tile * tile),
            name="rows",
        )(ids, *strips, inv0t, inv1t, lowt)

    def factor_cols(start, pieces, low):
        def at(offset):
            return pl.BlockSpec((1, tile, tile), lambda s: (s + offset, 0, 0))

        def kernel(*refs):
            cols_kernel(start, *refs)

        blocks = [at(offset) for _, offset in pieces]
        return pl.pallas_call(
            kernel,
            grid=(SUB // 2,),
            in_specs=[smem, *blocks, whole(inv_first), whole(inv_second), whole(low)],
            out_specs=pl.BlockSpec((2, 2 * width, tile), lambda s: (s, 0, 0)),
            out_shape=jax.ShapeDtypeStruct((SUB, 2 * width, tile), BF16),
            scratch_shapes=[pltpu.VMEM((2 * width, 2 * tile), BF16)],
            compiler_params=params(),
            cost_estimate=cost(SUB * 6 * tile * width * width, 24 * SUB * tile * tile),
            name="cols_%d" % start,
        )(ids, *[array for array, _ in pieces], inv_first, inv_second, low)

    def cost(flops, size):
        return pl.CostEstimate(flops=1, bytes_accessed=1, transcendentals=0)

    def clear():
        def place(i):
            group, first = 1, 0
            for g in range(1, groups):
                begin = ratio * g * (g - 1) // 2
                group = jnp.where(i >= begin, g, group)
                first = jnp.where(i >= begin, begin, first)
            return (i - first, 0, group, 0)

        return pl.pallas_call(
            zeros_kernel,
            grid=(ratio * groups * (groups - 1) // 2,),
            in_specs=[smem],
            out_specs=pl.BlockSpec((1, tile, SUB, tile), place),
            out_shape=jax.ShapeDtypeStruct(view.shape, BF16),
            compiler_params=params(),
            cost_estimate=cost(0, tiles * tile * SUB * tile * 2),
            name="clear",
        )(ids)

    def update(result, group, start, stop, cols, panels):
        grid_block = pl.BlockSpec((1, tile, SUB, tile), lambda t: (t + start, 0, group, 0))

        def kernel(*refs):
            update_kernel(group, start, *refs)

        return pl.pallas_call(
            kernel,
            grid=(stop - start,),
            in_specs=[
                smem,
                whole(cols),
                pl.BlockSpec((1, tile, 2 * width), lambda t: (t + start, 0, 0)),
                grid_block,
                pl.BlockSpec(memory_space=pl.ANY),
            ],
            out_specs=grid_block,
            out_shape=jax.ShapeDtypeStruct(view.shape, BF16),
            scratch_shapes=[pltpu.VMEM((tile // LANES, tile * SUB, LANES), F32)],
            input_output_aliases={4: 0},
            compiler_params=params(),
            cost_estimate=cost(
                (stop - start) * 2 * tile * tile * 2 * width * SUB,
                (stop - start) * 6 * tile * tile * SUB,
            ),
            name="update_%d_%d" % (group, start),
        )(ids, cols, panels, view, result)

    def cross(value):
        return move(value, lambda r, c: (4 + c, r - 4) if r >= 4 else None)

    half = SUB // 2
    held = jnp.swapaxes(view[0], 0, 1)
    even = [held[g * SUB : (g + 1) * SUB : 2] for g in range(groups)]
    odd = [held[g * SUB + 1 : (g + 1) * SUB : 2] for g in range(groups)]

    def pick(group, lifted, crossed):
        got = jnp.concatenate([lifted, crossed])
        return jnp.where(upper, got, jnp.concatenate([even[group], odd[group]]))

    def factor_group(group, base, over_y, over_z, even_zy, odd_zy):
        pieces = [(a, o) for a in (base, over_y, over_z) for o in (0, half)]
        return factor_cols(group * SUB, pieces + [even_zy, odd_zy], low)

    lift_0 = lift(even[0])
    strip = together(view, even[0])[0][:, :, 0, :]
    swapped = jnp.swapaxes(strip, 1, 2)
    cross_0 = cross(swapped[:half])
    result = clear()
    lift_0, cross_0, strip, swapped = together(lift_0, cross_0, strip, swapped)

    base_0 = pick(0, lift_0, cross_0)
    z_0, y_0 = across_z(base_0), across_y(base_0)
    strip_2 = across_x(strip)
    z_0, y_0, result, inv0t, inv1t, cross_0, lift_0 = together(z_0, y_0, result, inv0t, inv1t, cross_0, lift_0)

    first_zy = across_y(z_0[:1])
    both_0 = across_y(z_0)
    cross_1 = cross(together(swapped[half : 2 * half], cross_0)[0])
    lift_1 = lift(together(even[1], lift_0)[0])
    strip_1 = across_core(strip)
    mine = jnp.concatenate([base_0[:1], y_0[:1], z_0[:1], first_zy])
    other = across_core(mine)
    low, lowt = factor_link(mine, other)
    low, both_0, cross_1, lift_1, strip_1, strip_2 = together(low, both_0, cross_1, lift_1, strip_1, strip_2)

    base_1 = pick(1, lift_1, cross_1)
    z_1, y_1 = across_z(base_1), across_y(base_1)
    strip_3 = across_core(strip_2)
    cols_0 = factor_group(0, base_0, y_0, z_0, (both_0, 0), (both_0, half))
    panels = factor_rows((strip, strip_1, strip_2, strip_3), lowt)
    z_1, y_1, cols_0, panels = together(z_1, y_1, cols_0, panels)

    lift_2 = lift(together(even[2], z_1)[0])
    cross_2 = cross(together(swapped[2 * half :], z_1)[0])
    both_1 = across_y(z_1)
    result = update(result, 0, 0, tiles, cols_0, panels)
    lift_2, cross_2, both_1, result = together(lift_2, cross_2, both_1, result)

    base_2 = pick(2, lift_2, cross_2)
    z_2, y_2 = across_z(base_2), across_y(base_2)
    cols_1 = factor_group(1, base_1, y_1, z_1, (both_1, 0), (both_1, half))
    middle = 2 * ratio
    result = update(result, 1, ratio, middle, cols_1, panels)
    z_2, y_2, result = together(z_2, y_2, result)

    even_2, odd_2 = across_y(z_2[:half]), across_z(y_2[half:])
    result = update(result, 1, middle, tiles, cols_1, panels)
    even_2, odd_2, result = together(even_2, odd_2, result)
    cols_2 = factor_group(2, base_2, y_2, z_2, (even_2, 0), (odd_2, 0))
    result = update(result, 2, 2 * ratio, tiles, cols_2, panels)
    return panels.reshape(tiles, 1, tile, 2 * width), result.reshape(matrix.shape)


def fits(mesh, matrix, inv_first):
    tiles_match = matrix.shape[3] == 3 * SUB and matrix.shape[0] == 12
    panel_match = inv_first.shape[0] == 2 * matrix.shape[2]
    return mesh.shape["row"] == 8 and mesh.shape["col"] == 4 and tiles_match and panel_match


def solution(mesh):
    def body(matrix, inv_first, inv_second):
        plan = local if fits(mesh, matrix, inv_first) else local_any
        return plan(matrix, inv_first, inv_second)

    return jax.shard_map(
        body,
        mesh=mesh,
        in_specs=(P(None, "row", None, None, "col", None), P(), P()),
        out_specs=(P(None, "row", None, None), P(None, "row", None, None, "col", None)),
        check_vma=False,
    )
```

```python
import jax
import jax.numpy as jnp
from jax import lax
from jax.experimental import pallas as pl
from jax.experimental.pallas import tpu as pltpu
from jax.sharding import PartitionSpec as P

F32 = jnp.float32
BF16 = jnp.bfloat16
LANES = 128
SUB = 8
VMEM_LIMIT = 60 * 1024 * 1024


def from_root(value, axis, source):
    kept = jnp.where(lax.axis_index(axis) == source, value, 0).astype(value.dtype)
    return lax.psum(kept, axis)


def outer_minus(target, left_rows, right_rows):
    product = lax.dot_general(
        left_rows, right_rows, (((1,), (1,)), ((), ())), preferred_element_type=jnp.float32
    )
    return (target.astype(jnp.float32) - product).astype(jnp.bfloat16)


def panel_columns(first_tile, step_index):
    halves = []
    for half_index in range(2):
        halves.append(from_root(first_tile, "col", 2 * step_index + half_index))
    return jnp.concatenate(halves, axis=1)


def column_factor(row_factor, col_id, row_count, col_count):
    owner_count = row_count // col_count
    received = []
    for owner_slot in range(owner_count):
        received.append(from_root(row_factor, "row", owner_slot * col_count + col_id))
    gathered = jnp.stack(received, axis=1)
    return gathered.reshape(-1, gathered.shape[-1])


def local_any(matrix, inv_first, inv_second):
    row_count = lax.axis_size("row")
    col_count = lax.axis_size("col")
    row_id = lax.axis_index("row")
    col_id = lax.axis_index("col")
    tile_rows = matrix.shape[0]
    tile_size = matrix.shape[2]
    tile_cols = matrix.shape[3]
    width = inv_first.shape[0]
    local_rows = tile_rows * tile_size
    local_cols = tile_cols * tile_size
    current = matrix.reshape(local_rows, local_cols)
    row_position = jnp.arange(local_rows, dtype=jnp.int32)
    global_rows = (
        row_position // tile_size * row_count + row_id
    ) * tile_size + row_position % tile_size
    col_position = jnp.arange(local_cols, dtype=jnp.int32)
    global_cols = (
        col_position // tile_size * col_count + col_id
    ) * tile_size + col_position % tile_size

    def factor_rows(first_tile, inverse, step_index):
        columns = panel_columns(first_tile, step_index)
        product = lax.dot_general(
            columns, inverse, (((1,), (1,)), ((), ())), preferred_element_type=jnp.float32
        )
        keep_rows = (global_rows >= (step_index + 1) * width)[:, None]
        return jnp.where(keep_rows, product, jnp.zeros_like(product)).astype(jnp.bfloat16)

    def spread_columns(row_factor):
        shaped = row_factor.reshape(tile_rows, tile_size, width)
        return column_factor(shaped, col_id, row_count, col_count)

    row_first = factor_rows(current[:, :tile_size], inv_first, 0)
    col_first = spread_columns(row_first)
    updated = outer_minus(current, row_first, col_first)
    row_second = factor_rows(updated[:, :tile_size], inv_second, 1)
    col_second = spread_columns(row_second)
    result = outer_minus(updated, row_second, col_second)
    row_tiles = global_rows // tile_size
    col_tiles = global_cols // tile_size
    keep_mask = (
        (global_rows >= 2 * width)[:, None]
        & (global_cols >= 2 * width)[None, :]
        & (row_tiles[:, None] >= col_tiles[None, :])
    )
    trailing = jnp.where(keep_mask, result, jnp.zeros_like(result))
    panels = jnp.concatenate([row_first, row_second], axis=1)
    return (panels.reshape(tile_rows, 1, tile_size, 2 * width), trailing.reshape(matrix.shape))


def dot(left, right):
    return lax.dot_general(left, right, (((1,), (0,)), ((), ())), preferred_element_type=F32)


def link_kernel(ids, mine, other, inv0t, low, lowt):
    slot, plane, core = ids[0] % 4, ids[1] // 2, ids[1] % 2
    tile = mine.shape[1]

    def piece(panel_tile, owner):
        held = slot ^ panel_tile
        return jnp.where(core == owner, mine[held].astype(F32), other[held].astype(F32))

    @pl.when(plane == 0)
    def _():
        rows = [jnp.concatenate([piece(2 + i, j) for j in range(2)], axis=1) for i in range(2)]
        block = jnp.concatenate(rows, axis=0)
        result = dot(block.astype(BF16), inv0t[...])
        low[...] = result.astype(BF16)
        lowt[...] = result.T.astype(BF16)

    @pl.when(plane == 1)
    def _():
        rows = [jnp.concatenate([piece(j, i) for i in range(2)], axis=1) for j in range(2)]
        block = jnp.concatenate(rows, axis=0).T
        result = dot(block.astype(BF16), inv0t[...])
        low[...] = result.astype(BF16)
        lowt[...] = result.T.astype(BF16)


def rows_kernel(ids, q0, q1, q2, q3, inv0t, inv1t, lowt, out, buf):
    count, tile, _ = q0.shape
    width = 2 * tile
    row_id, col_id = ids[0], ids[1]
    for m, ref in enumerate((q0, q1, q2, q3)):
        base = pl.multiple_of((col_id ^ m) * tile, tile)
        for i in range(count):
            buf[i * tile : (i + 1) * tile, pl.ds(base, tile)] = ref[i]
    local = lax.broadcasted_iota(jnp.int32, (count * tile, 1), 0) // tile
    tile_row = (pl.program_id(0) * count + local) * 8 + row_id
    first = dot(buf[:, :width], inv0t[...])
    first = jnp.where(tile_row >= 2, first, 0.0).astype(BF16)
    rest = (buf[:, width:].astype(F32) - dot(first, lowt[...])).astype(BF16)
    second = dot(rest, inv1t[...])
    second = jnp.where(tile_row >= 4, second, 0.0).astype(BF16)
    for i in range(count):
        out[i, :, :width] = first[i * tile : (i + 1) * tile]
        out[i, :, width:] = second[i * tile : (i + 1) * tile]


def cols_kernel(start, ids, *refs):
    pieces, (inv0, inv1, low, out, raw) = refs[:8], refs[8:]
    tile = pieces[0].shape[1]
    width = 2 * tile
    row_id, col_id = ids[0], ids[1]
    for m in range(4):
        base = pl.multiple_of(((row_id % 4) ^ m) * tile, tile)
        for i in range(2):
            raw[pl.ds(base, tile), i * tile : (i + 1) * tile] = pieces[2 * m + i][0]
    local = lax.broadcasted_iota(jnp.int32, (1, 2 * tile), 1) // tile
    tile_col = (start + pl.program_id(0) * 2 + local) * 4 + col_id
    first = dot(inv0[...], raw[:width])
    first = jnp.where(tile_col >= 2, first, 0.0).astype(BF16)
    rest = (raw[width:].astype(F32) - dot(low[...], first)).astype(BF16)
    second = dot(inv1[...], rest)
    second = jnp.where(tile_col >= 4, second, 0.0).astype(BF16)
    for i in range(2):
        out[i, :width] = first[:, i * tile : (i + 1) * tile]
        out[i, width:] = second[:, i * tile : (i + 1) * tile]


def zeros_kernel(_, out):
    out[...] = jnp.zeros_like(out)


def update_kernel(group, start, ids, cols, factor, matrix, _, out, acc):
    tile = factor.shape[1]
    row_id, col_id = ids[0], ids[1]
    tile_row = (start + pl.program_id(0)) * 8 + row_id
    end = jnp.where(tile_row >= 4, (tile_row - col_id) // 4 + 1 - group * SUB, 0)
    begin = 1 if group == 0 else 0

    @pl.when(end <= begin)
    def _():
        out[...] = jnp.zeros_like(out)

    @pl.when(end > begin)
    def _():
        def fill(chosen):
            for s in chosen:
                product = dot(factor[0], cols[s])
                for part in range(tile // LANES):
                    lanes = slice(part * LANES, (part + 1) * LANES)
                    acc[part, pl.ds(s, tile, stride=SUB), :] = product[:, lanes]

        @pl.when(end >= SUB)
        def _():
            fill(range(begin, SUB))

        for pair in range(0, SUB, 2):

            @pl.when((end < SUB) & (pair < end))
            def _(pair=pair):
                fill(range(max(pair, begin), pair + 2))

        some = 32
        sub = lax.broadcasted_iota(jnp.int32, (some, SUB, LANES), 1)
        keep = (sub >= begin) & (sub < end)

        def finish(i, carry):
            at = pl.multiple_of(i * some, some)
            span = pl.ds(pl.multiple_of(at * SUB, some * SUB), some * SUB)
            for part in range(tile // LANES):
                lanes = slice(part * LANES, (part + 1) * LANES)
                product = acc[part, span, :].reshape(some, SUB, LANES)
                value = matrix[0, pl.ds(at, some), :, lanes].astype(F32) - product
                out[0, pl.ds(at, some), :, lanes] = jnp.where(keep, value, 0.0).astype(BF16)
            return carry

        lax.fori_loop(0, tile // some, finish, 0)


def params():
    return pltpu.CompilerParams(vmem_limit_bytes=VMEM_LIMIT)


def whole(array):
    rank = array.ndim
    return pl.BlockSpec(array.shape, lambda *_: (0,) * rank)


def local(matrix, inv_first, inv_second):
    row_id = lax.axis_index("row")
    col_id = lax.axis_index("col")
    ids = jnp.stack([row_id, col_id]).astype(jnp.int32)
    tiles, _, tile, tile_cols, _, _ = matrix.shape
    width = inv_first.shape[0]
    groups = tile_cols // SUB
    ratio = tiles // groups
    view = matrix.reshape(tiles, tile, tile_cols, tile)
    upper = row_id >= 4
    smem = pl.BlockSpec(memory_space=pltpu.SMEM)
    inv0t, inv1t = inv_first.T, inv_second.T

    def together(*values):
        return lax.optimization_barrier(values)

    def move(value, target):
        pairs = []
        for r in range(8):
            for c in range(4):
                to = target(r, c)
                if to is not None:
                    pairs.append((r * 4 + c, to[0] * 4 + to[1]))
        return lax.ppermute(value, ("row", "col"), pairs)

    def across_z(value):
        return move(value, lambda r, c: (r ^ 2, c))

    def across_y(value):
        return move(value, lambda r, c: (r ^ 1, c))

    def across_core(value):
        return move(value, lambda r, c: (r, c ^ 1))

    def across_x(value):
        return move(value, lambda r, c: (r, c ^ 2))

    def lift(value):
        return move(value, lambda r, c: (r + 4, c) if r < 4 else None)

    def factor_link(mine, other):
        square = jax.ShapeDtypeStruct((width, width), BF16)
        return pl.pallas_call(
            link_kernel,
            in_specs=[smem, whole(mine), whole(other), whole(inv0t)],
            out_specs=[whole(square), whole(square)],
            out_shape=[square, square],
            grid=(1,),
            compiler_params=params(),
            name="link",
        )(ids, mine, other, inv0t)

    def factor_rows(strips, lowt):
        count = 2
        block = pl.BlockSpec((count, tile, tile), lambda t: (t, 0, 0))
        return pl.pallas_call(
            rows_kernel,
            grid=(tiles // count,),
            in_specs=[smem, *[block] * 4, whole(inv0t), whole(inv1t), whole(lowt)],
            out_specs=pl.BlockSpec((count, tile, 2 * width), lambda t: (t, 0, 0)),
            out_shape=jax.ShapeDtypeStruct((tiles, tile, 2 * width), BF16),
            scratch_shapes=[pltpu.VMEM((count * tile, 2 * width), BF16)],
            compiler_params=params(),
            cost_estimate=cost(tiles * 6 * tile * width * width, 24 * tiles * tile * tile),
            name="rows",
        )(ids, *strips, inv0t, inv1t, lowt)

    def factor_cols(start, pieces, low):
        def at(offset):
            return pl.BlockSpec((1, tile, tile), lambda s: (s + offset, 0, 0))

        def kernel(*refs):
            cols_kernel(start, *refs)

        blocks = [at(offset) for _, offset in pieces]
        return pl.pallas_call(
            kernel,
            grid=(SUB // 2,),
            in_specs=[smem, *blocks, whole(inv_first), whole(inv_second), whole(low)],
            out_specs=pl.BlockSpec((2, 2 * width, tile), lambda s: (s, 0, 0)),
            out_shape=jax.ShapeDtypeStruct((SUB, 2 * width, tile), BF16),
            scratch_shapes=[pltpu.VMEM((2 * width, 2 * tile), BF16)],
            compiler_params=params(),
            cost_estimate=cost(SUB * 6 * tile * width * width, 24 * SUB * tile * tile),
            name="cols_%d" % start,
        )(ids, *[array for array, _ in pieces], inv_first, inv_second, low)

    def cost(flops, size):
        return pl.CostEstimate(flops=flops, bytes_accessed=size, transcendentals=0)

    def clear(gate):
        def place(i):
            group, first = 1, 0
            for g in range(1, groups):
                begin = ratio * g * (g - 1) // 2
                group = jnp.where(i >= begin, g, group)
                first = jnp.where(i >= begin, begin, first)
            return (i - first, 0, group, 0)

        return pl.pallas_call(
            zeros_kernel,
            grid=(ratio * groups * (groups - 1) // 2,),
            in_specs=[smem],
            out_specs=pl.BlockSpec((1, tile, SUB, tile), place),
            out_shape=jax.ShapeDtypeStruct(view.shape, BF16),
            compiler_params=params(),
            cost_estimate=cost(0, tiles * tile * SUB * tile * 2),
            name="clear",
        )(together(ids, gate)[0])

    def update(result, group, start, stop, cols, panels):
        grid_block = pl.BlockSpec((1, tile, SUB, tile), lambda t: (t + start, 0, group, 0))

        def kernel(*refs):
            update_kernel(group, start, *refs)

        return pl.pallas_call(
            kernel,
            grid=(stop - start,),
            in_specs=[
                smem,
                whole(cols),
                pl.BlockSpec((1, tile, 2 * width), lambda t: (t + start, 0, 0)),
                grid_block,
                pl.BlockSpec(memory_space=pl.ANY),
            ],
            out_specs=grid_block,
            out_shape=jax.ShapeDtypeStruct(view.shape, BF16),
            scratch_shapes=[pltpu.VMEM((tile // LANES, tile * SUB, LANES), F32)],
            input_output_aliases={4: 0},
            compiler_params=params(),
            cost_estimate=cost(
                (stop - start) * 2 * tile * tile * 2 * width * SUB,
                (stop - start) * 6 * tile * tile * SUB,
            ),
            name="update_%d_%d" % (group, start),
        )(ids, cols, panels, view, result)

    def cross(value):
        return move(value, lambda r, c: (4 + c, r - 4) if r >= 4 else None)

    half = SUB // 2
    held = jnp.swapaxes(view[0], 0, 1)
    even = [held[g * SUB : (g + 1) * SUB : 2] for g in range(groups)]
    odd = [held[g * SUB + 1 : (g + 1) * SUB : 2] for g in range(groups)]

    def pick(group, lifted, crossed):
        got = jnp.concatenate([lifted, crossed])
        return jnp.where(upper, got, jnp.concatenate([even[group], odd[group]]))

    def factor_group(group, base, over_y, over_z, even_zy, odd_zy):
        pieces = [(a, o) for a in (base, over_y, over_z) for o in (0, half)]
        return factor_cols(group * SUB, pieces + [even_zy, odd_zy], low)

    lift_0 = lift(even[0])
    strip_a = together(view, even[0])[0][:half, :, 0, :]
    cross_0 = cross(jnp.swapaxes(strip_a, 1, 2))
    lift_0, cross_0, source, inv0t, inv1t = together(lift_0, cross_0, view, inv0t, inv1t)

    base_0 = pick(0, lift_0, cross_0)
    z_0, y_0 = across_z(base_0), across_y(base_0)
    strip_b = source[half:, :, 0, :]
    swapped = jnp.swapaxes(strip_b, 1, 2)
    strip = jnp.concatenate([strip_a, strip_b])
    strip_2 = across_x(strip)
    z_0, y_0, cross_0, lift_0, swapped = together(z_0, y_0, cross_0, lift_0, swapped)

    both_0 = across_y(z_0)
    cross_1 = cross(together(swapped[:half], cross_0)[0])
    lift_1 = lift(together(even[1], lift_0)[0])
    strip_1 = across_core(strip)
    result = clear(z_0)
    both_0, cross_1, lift_1, strip_1, strip_2, result = together(both_0, cross_1, lift_1, strip_1, strip_2, result)

    mine = jnp.concatenate([base_0[:1], y_0[:1], z_0[:1], both_0[:1]])
    other = across_core(mine)
    low, lowt = factor_link(mine, other)
    base_1 = pick(1, lift_1, cross_1)
    z_1, y_1 = across_z(base_1), across_y(base_1)
    strip_3 = across_core(strip_2)
    cols_0 = factor_group(0, base_0, y_0, z_0, (both_0, 0), (both_0, half))
    panels = factor_rows((strip, strip_1, strip_2, strip_3), lowt)
    z_1, y_1, cols_0, panels = together(z_1, y_1, cols_0, panels)

    lift_2 = lift(together(even[2], z_1)[0])
    cross_2 = cross(together(swapped[half:], z_1)[0])
    both_1 = across_y(z_1)
    result = update(result, 0, 0, tiles, cols_0, panels)
    lift_2, cross_2, both_1, result = together(lift_2, cross_2, both_1, result)

    base_2 = pick(2, lift_2, cross_2)
    z_2, y_2 = across_z(base_2), across_y(base_2)
    cols_1 = factor_group(1, base_1, y_1, z_1, (both_1, 0), (both_1, half))
    middle = 2 * ratio
    result = update(result, 1, ratio, middle, cols_1, panels)
    z_2, y_2, result = together(z_2, y_2, result)

    even_2, odd_2 = across_y(z_2[:half]), across_z(y_2[half:])
    result = update(result, 1, middle, tiles, cols_1, panels)
    even_2, odd_2, result = together(even_2, odd_2, result)
    cols_2 = factor_group(2, base_2, y_2, z_2, (even_2, 0), (odd_2, 0))
    result = update(result, 2, 2 * ratio, tiles, cols_2, panels)
    return panels.reshape(tiles, 1, tile, 2 * width), result.reshape(matrix.shape)


def fits(mesh, matrix, inv_first):
    tiles_match = matrix.shape[3] == 3 * SUB and matrix.shape[0] == 12
    panel_match = inv_first.shape[0] == 2 * matrix.shape[2]
    return mesh.shape["row"] == 8 and mesh.shape["col"] == 4 and tiles_match and panel_match


def solution(mesh):
    def body(matrix, inv_first, inv_second):
        plan = local if fits(mesh, matrix, inv_first) else local_any
        return plan(matrix, inv_first, inv_second)

    return jax.shard_map(
        body,
        mesh=mesh,
        in_specs=(P(None, "row", None, None, "col", None), P(), P()),
        out_specs=(P(None, "row", None, None), P(None, "row", None, None, "col", None)),
        check_vma=False,
    )
```

```python
import jax
import jax.numpy as jnp
from jax import lax
from jax.experimental import pallas as pl
from jax.experimental.pallas import tpu as pltpu
from jax.sharding import PartitionSpec as P

F32 = jnp.float32
BF16 = jnp.bfloat16
LANES = 128
SUB = 8
VMEM_LIMIT = 60 * 1024 * 1024


def from_root(value, axis, source):
    kept = jnp.where(lax.axis_index(axis) == source, value, 0).astype(value.dtype)
    return lax.psum(kept, axis)


def outer_minus(target, left_rows, right_rows):
    product = lax.dot_general(
        left_rows, right_rows, (((1,), (1,)), ((), ())), preferred_element_type=jnp.float32
    )
    return (target.astype(jnp.float32) - product).astype(jnp.bfloat16)


def panel_columns(first_tile, step_index):
    halves = []
    for half_index in range(2):
        halves.append(from_root(first_tile, "col", 2 * step_index + half_index))
    return jnp.concatenate(halves, axis=1)


def column_factor(row_factor, col_id, row_count, col_count):
    owner_count = row_count // col_count
    received = []
    for owner_slot in range(owner_count):
        received.append(from_root(row_factor, "row", owner_slot * col_count + col_id))
    gathered = jnp.stack(received, axis=1)
    return gathered.reshape(-1, gathered.shape[-1])


def local_any(matrix, inv_first, inv_second):
    row_count = lax.axis_size("row")
    col_count = lax.axis_size("col")
    row_id = lax.axis_index("row")
    col_id = lax.axis_index("col")
    tile_rows = matrix.shape[0]
    tile_size = matrix.shape[2]
    tile_cols = matrix.shape[3]
    width = inv_first.shape[0]
    local_rows = tile_rows * tile_size
    local_cols = tile_cols * tile_size
    current = matrix.reshape(local_rows, local_cols)
    row_position = jnp.arange(local_rows, dtype=jnp.int32)
    global_rows = (
        row_position // tile_size * row_count + row_id
    ) * tile_size + row_position % tile_size
    col_position = jnp.arange(local_cols, dtype=jnp.int32)
    global_cols = (
        col_position // tile_size * col_count + col_id
    ) * tile_size + col_position % tile_size

    def factor_rows(first_tile, inverse, step_index):
        columns = panel_columns(first_tile, step_index)
        product = lax.dot_general(
            columns, inverse, (((1,), (1,)), ((), ())), preferred_element_type=jnp.float32
        )
        keep_rows = (global_rows >= (step_index + 1) * width)[:, None]
        return jnp.where(keep_rows, product, jnp.zeros_like(product)).astype(jnp.bfloat16)

    def spread_columns(row_factor):
        shaped = row_factor.reshape(tile_rows, tile_size, width)
        return column_factor(shaped, col_id, row_count, col_count)

    row_first = factor_rows(current[:, :tile_size], inv_first, 0)
    col_first = spread_columns(row_first)
    updated = outer_minus(current, row_first, col_first)
    row_second = factor_rows(updated[:, :tile_size], inv_second, 1)
    col_second = spread_columns(row_second)
    result = outer_minus(updated, row_second, col_second)
    row_tiles = global_rows // tile_size
    col_tiles = global_cols // tile_size
    keep_mask = (
        (global_rows >= 2 * width)[:, None]
        & (global_cols >= 2 * width)[None, :]
        & (row_tiles[:, None] >= col_tiles[None, :])
    )
    trailing = jnp.where(keep_mask, result, jnp.zeros_like(result))
    panels = jnp.concatenate([row_first, row_second], axis=1)
    return (panels.reshape(tile_rows, 1, tile_size, 2 * width), trailing.reshape(matrix.shape))


def dot(left, right):
    return lax.dot_general(left, right, (((1,), (0,)), ((), ())), preferred_element_type=F32)


def link_kernel(ids, mine, other, inv0t, low, lowt):
    slot, plane, core = ids[0] % 4, ids[1] // 2, ids[1] % 2
    tile = mine.shape[1]

    def piece(panel_tile, owner):
        held = slot ^ panel_tile
        return jnp.where(core == owner, mine[held].astype(F32), other[held].astype(F32))

    @pl.when(plane == 0)
    def _():
        rows = [jnp.concatenate([piece(2 + i, j) for j in range(2)], axis=1) for i in range(2)]
        block = jnp.concatenate(rows, axis=0)
        result = dot(block.astype(BF16), inv0t[...])
        low[...] = result.astype(BF16)
        lowt[...] = result.T.astype(BF16)

    @pl.when(plane == 1)
    def _():
        rows = [jnp.concatenate([piece(j, i) for i in range(2)], axis=1) for j in range(2)]
        block = jnp.concatenate(rows, axis=0).T
        result = dot(block.astype(BF16), inv0t[...])
        low[...] = result.astype(BF16)
        lowt[...] = result.T.astype(BF16)


def rows_kernel(ids, q0, q1, q2, q3, inv0t, inv1t, lowt, out, buf):
    count, tile, _ = q0.shape
    width = 2 * tile
    row_id, col_id = ids[0], ids[1]
    for m, ref in enumerate((q0, q1, q2, q3)):
        base = pl.multiple_of((col_id ^ m) * tile, tile)
        for i in range(count):
            buf[i * tile : (i + 1) * tile, pl.ds(base, tile)] = ref[i]
    local = lax.broadcasted_iota(jnp.int32, (count * tile, 1), 0) // tile
    tile_row = (pl.program_id(0) * count + local) * 8 + row_id
    first = dot(buf[:, :width], inv0t[...])
    first = jnp.where(tile_row >= 2, first, 0.0).astype(BF16)
    rest = (buf[:, width:].astype(F32) - dot(first, lowt[...])).astype(BF16)
    second = dot(rest, inv1t[...])
    second = jnp.where(tile_row >= 4, second, 0.0).astype(BF16)
    for i in range(count):
        out[i, :, :width] = first[i * tile : (i + 1) * tile]
        out[i, :, width:] = second[i * tile : (i + 1) * tile]


def cols_kernel(start, ids, *refs):
    pieces, (inv0, inv1, low, out, raw) = refs[:8], refs[8:]
    count, tile = 2 * pieces[0].shape[0], pieces[0].shape[1]
    width = 2 * tile
    row_id, col_id = ids[0], ids[1]
    for m in range(4):
        base = pl.multiple_of(((row_id % 4) ^ m) * tile, tile)
        for i in range(count):
            raw[pl.ds(base, tile), i * tile : (i + 1) * tile] = pieces[2 * m + i % 2][i // 2]
    local = lax.broadcasted_iota(jnp.int32, (1, count * tile), 1) // tile
    tile_col = (start + pl.program_id(0) * count + local) * 4 + col_id
    first = dot(inv0[...], raw[:width])
    first = jnp.where(tile_col >= 2, first, 0.0).astype(BF16)
    rest = (raw[width:].astype(F32) - dot(low[...], first)).astype(BF16)
    second = dot(inv1[...], rest)
    second = jnp.where(tile_col >= 4, second, 0.0).astype(BF16)
    for i in range(count):
        out[i, :width] = first[:, i * tile : (i + 1) * tile]
        out[i, width:] = second[:, i * tile : (i + 1) * tile]


def zeros_kernel(_, out):
    out[...] = jnp.zeros_like(out)


def update_kernel(group, start, ids, cols, factor, matrix, _, out, acc):
    tile = factor.shape[1]
    row_id, col_id = ids[0], ids[1]
    tile_row = (start + pl.program_id(0)) * 8 + row_id
    end = jnp.where(tile_row >= 4, (tile_row - col_id) // 4 + 1 - group * SUB, 0)
    begin = 1 if group == 0 else 0

    @pl.when(end <= begin)
    def _():
        out[...] = jnp.zeros_like(out)

    @pl.when(end > begin)
    def _():
        def fill(chosen):
            for s in chosen:
                product = dot(factor[0], cols[s])
                for part in range(tile // LANES):
                    lanes = slice(part * LANES, (part + 1) * LANES)
                    acc[part, pl.ds(s, tile, stride=SUB), :] = product[:, lanes]

        @pl.when(end >= SUB)
        def _():
            fill(range(begin, SUB))

        for pair in range(0, SUB, 2):

            @pl.when((end < SUB) & (pair < end))
            def _(pair=pair):
                fill(range(max(pair, begin), pair + 2))

        some = 32
        sub = lax.broadcasted_iota(jnp.int32, (some, SUB, LANES), 1)
        keep = (sub >= begin) & (sub < end)

        def finish(i, carry):
            at = pl.multiple_of(i * some, some)
            span = pl.ds(pl.multiple_of(at * SUB, some * SUB), some * SUB)
            for part in range(tile // LANES):
                lanes = slice(part * LANES, (part + 1) * LANES)
                product = acc[part, span, :].reshape(some, SUB, LANES)
                value = matrix[0, pl.ds(at, some), :, lanes].astype(F32) - product
                out[0, pl.ds(at, some), :, lanes] = jnp.where(keep, value, 0.0).astype(BF16)
            return carry

        lax.fori_loop(0, tile // some, finish, 0)


def params():
    return pltpu.CompilerParams(vmem_limit_bytes=VMEM_LIMIT)


def whole(array):
    rank = array.ndim
    return pl.BlockSpec(array.shape, lambda *_: (0,) * rank)


def local(matrix, inv_first, inv_second):
    row_id = lax.axis_index("row")
    col_id = lax.axis_index("col")
    ids = jnp.stack([row_id, col_id]).astype(jnp.int32)
    tiles, _, tile, tile_cols, _, _ = matrix.shape
    width = inv_first.shape[0]
    groups = tile_cols // SUB
    ratio = tiles // groups
    view = matrix.reshape(tiles, tile, tile_cols, tile)
    upper = row_id >= 4
    smem = pl.BlockSpec(memory_space=pltpu.SMEM)
    inv0t, inv1t = inv_first.T, inv_second.T

    def together(*values):
        return lax.optimization_barrier(values)

    def move(value, target):
        pairs = []
        for r in range(8):
            for c in range(4):
                to = target(r, c)
                if to is not None:
                    pairs.append((r * 4 + c, to[0] * 4 + to[1]))
        return lax.ppermute(value, ("row", "col"), pairs)

    def across_z(value):
        return move(value, lambda r, c: (r ^ 2, c))

    def across_y(value):
        return move(value, lambda r, c: (r ^ 1, c))

    def across_core(value):
        return move(value, lambda r, c: (r, c ^ 1))

    def across_x(value):
        return move(value, lambda r, c: (r, c ^ 2))

    def lift(value):
        return move(value, lambda r, c: (r + 4, c) if r < 4 else None)

    def factor_link(mine, other):
        square = jax.ShapeDtypeStruct((width, width), BF16)
        return pl.pallas_call(
            link_kernel,
            in_specs=[smem, whole(mine), whole(other), whole(inv0t)],
            out_specs=[whole(square), whole(square)],
            out_shape=[square, square],
            grid=(1,),
            compiler_params=params(),
            name="link",
        )(ids, mine, other, inv0t)

    def factor_rows(strips, lowt):
        count = 2
        block = pl.BlockSpec((count, tile, tile), lambda t: (t, 0, 0))
        return pl.pallas_call(
            rows_kernel,
            grid=(tiles // count,),
            in_specs=[smem, *[block] * 4, whole(inv0t), whole(inv1t), whole(lowt)],
            out_specs=pl.BlockSpec((count, tile, 2 * width), lambda t: (t, 0, 0)),
            out_shape=jax.ShapeDtypeStruct((tiles, tile, 2 * width), BF16),
            scratch_shapes=[pltpu.VMEM((count * tile, 2 * width), BF16)],
            compiler_params=params(),
            cost_estimate=cost(tiles * 6 * tile * width * width, 24 * tiles * tile * tile),
            name="rows",
        )(ids, *strips, inv0t, inv1t, lowt)

    def factor_cols(start, pieces, low):
        def at(offset):
            return pl.BlockSpec((2, tile, tile), lambda s: (s + offset // 2, 0, 0))

        def kernel(*refs):
            cols_kernel(start, *refs)

        blocks = [at(offset) for _, offset in pieces]
        return pl.pallas_call(
            kernel,
            grid=(SUB // 4,),
            in_specs=[smem, *blocks, whole(inv_first), whole(inv_second), whole(low)],
            out_specs=pl.BlockSpec((4, 2 * width, tile), lambda s: (s, 0, 0)),
            out_shape=jax.ShapeDtypeStruct((SUB, 2 * width, tile), BF16),
            scratch_shapes=[pltpu.VMEM((2 * width, 4 * tile), BF16)],
            compiler_params=params(),
            cost_estimate=cost(SUB * 6 * tile * width * width, 24 * SUB * tile * tile),
            name="cols_%d" % start,
        )(ids, *[array for array, _ in pieces], inv_first, inv_second, low)

    def cost(flops, size):
        return pl.CostEstimate(flops=flops, bytes_accessed=size, transcendentals=0)

    def clear(gate):
        def place(i):
            group, first = 1, 0
            for g in range(1, groups):
                begin = ratio * g * (g - 1) // 2
                group = jnp.where(i >= begin, g, group)
                first = jnp.where(i >= begin, begin, first)
            return (i - first, 0, group, 0)

        return pl.pallas_call(
            zeros_kernel,
            grid=(ratio * groups * (groups - 1) // 2,),
            in_specs=[smem],
            out_specs=pl.BlockSpec((1, tile, SUB, tile), place),
            out_shape=jax.ShapeDtypeStruct(view.shape, BF16),
            compiler_params=params(),
            cost_estimate=cost(0, tiles * tile * SUB * tile * 2),
            name="clear",
        )(together(ids, gate)[0])

    def update(result, group, start, stop, cols, panels):
        grid_block = pl.BlockSpec((1, tile, SUB, tile), lambda t: (t + start, 0, group, 0))

        def kernel(*refs):
            update_kernel(group, start, *refs)

        return pl.pallas_call(
            kernel,
            grid=(stop - start,),
            in_specs=[
                smem,
                whole(cols),
                pl.BlockSpec((1, tile, 2 * width), lambda t: (t + start, 0, 0)),
                grid_block,
                pl.BlockSpec(memory_space=pl.ANY),
            ],
            out_specs=grid_block,
            out_shape=jax.ShapeDtypeStruct(view.shape, BF16),
            scratch_shapes=[pltpu.VMEM((tile // LANES, tile * SUB, LANES), F32)],
            input_output_aliases={4: 0},
            compiler_params=params(),
            cost_estimate=cost(
                (stop - start) * 2 * tile * tile * 2 * width * SUB,
                (stop - start) * 6 * tile * tile * SUB,
            ),
            name="update_%d_%d" % (group, start),
        )(ids, cols, panels, view, result)

    def cross(value):
        return move(value, lambda r, c: (4 + c, r - 4) if r >= 4 else None)

    half = SUB // 2
    held = jnp.swapaxes(view[0], 0, 1)
    even = [held[g * SUB : (g + 1) * SUB : 2] for g in range(groups)]
    odd = [held[g * SUB + 1 : (g + 1) * SUB : 2] for g in range(groups)]

    def pick(group, lifted, crossed):
        got = jnp.concatenate([lifted, crossed])
        return jnp.where(upper, got, jnp.concatenate([even[group], odd[group]]))

    def factor_group(group, base, over_y, over_z, even_zy, odd_zy):
        pieces = [(a, o) for a in (base, over_y, over_z) for o in (0, half)]
        return factor_cols(group * SUB, pieces + [even_zy, odd_zy], low)

    lift_0 = lift(even[0])
    strip_a = together(view, even[0])[0][:half, :, 0, :]
    cross_0 = cross(jnp.swapaxes(strip_a, 1, 2))
    lift_0, cross_0, source, inv0t, inv1t = together(lift_0, cross_0, view, inv0t, inv1t)

    base_0 = pick(0, lift_0, cross_0)
    z_0, y_0 = across_z(base_0), across_y(base_0)
    strip_b = source[half:, :, 0, :]
    swapped = jnp.swapaxes(strip_b, 1, 2)
    strip = jnp.concatenate([strip_a, strip_b])
    strip_2 = across_x(strip)
    z_0, y_0, cross_0, lift_0, swapped = together(z_0, y_0, cross_0, lift_0, swapped)

    both_0 = across_y(z_0)
    cross_1 = cross(together(swapped[:half], cross_0)[0])
    lift_1 = lift(together(even[1], lift_0)[0])
    strip_1 = across_core(strip)
    result = clear(z_0)
    both_0, cross_1, lift_1, strip_1, strip_2, result = together(both_0, cross_1, lift_1, strip_1, strip_2, result)

    mine = jnp.concatenate([base_0[:1], y_0[:1], z_0[:1], both_0[:1]])
    other = across_core(mine)
    low, lowt = factor_link(mine, other)
    base_1 = pick(1, lift_1, cross_1)
    z_1, y_1 = across_z(base_1), across_y(base_1)
    strip_3 = across_core(strip_2)
    cols_0 = factor_group(0, base_0, y_0, z_0, (both_0, 0), (both_0, half))
    panels = factor_rows((strip, strip_1, strip_2, strip_3), lowt)
    z_1, y_1, cols_0, panels = together(z_1, y_1, cols_0, panels)

    lift_2 = lift(together(even[2], z_1)[0])
    cross_2 = cross(together(swapped[half:], z_1)[0])
    both_1 = across_y(z_1)
    result = update(result, 0, 0, tiles, cols_0, panels)
    lift_2, cross_2, both_1, result = together(lift_2, cross_2, both_1, result)

    base_2 = pick(2, lift_2, cross_2)
    z_2, y_2 = across_z(base_2), across_y(base_2)
    cols_1 = factor_group(1, base_1, y_1, z_1, (both_1, 0), (both_1, half))
    middle = 2 * ratio
    result = update(result, 1, ratio, middle, cols_1, panels)
    z_2, y_2, result = together(z_2, y_2, result)

    even_2, odd_2 = across_y(z_2[:half]), across_z(y_2[half:])
    result = update(result, 1, middle, tiles, cols_1, panels)
    even_2, odd_2, result = together(even_2, odd_2, result)
    cols_2 = factor_group(2, base_2, y_2, z_2, (even_2, 0), (odd_2, 0))
    result = update(result, 2, 2 * ratio, tiles, cols_2, panels)
    return panels.reshape(tiles, 1, tile, 2 * width), result.reshape(matrix.shape)


def fits(mesh, matrix, inv_first):
    tiles_match = matrix.shape[3] == 3 * SUB and matrix.shape[0] == 12
    panel_match = inv_first.shape[0] == 2 * matrix.shape[2]
    return mesh.shape["row"] == 8 and mesh.shape["col"] == 4 and tiles_match and panel_match


def solution(mesh):
    def body(matrix, inv_first, inv_second):
        plan = local if fits(mesh, matrix, inv_first) else local_any
        return plan(matrix, inv_first, inv_second)

    return jax.shard_map(
        body,
        mesh=mesh,
        in_specs=(P(None, "row", None, None, "col", None), P(), P()),
        out_specs=(P(None, "row", None, None), P(None, "row", None, None, "col", None)),
        check_vma=False,
    )
```
